32 devices in a mesh: dp: 2 (over x), expert: 8 (over z, y), tensor: 2 (over core).
Axes of the slice: x: 2, y: 2, z: 4, core: 2. Of those that a mesh axis runs over, the one named last changes fastest.
Arguments:
- upstream: bfloat16 [2048, 2880], P(('dp', 'expert'), 'tensor'), may hold values from -3 to 3
- expert_ids: int32 [2048, 4], P(('dp', 'expert')), may hold values from 0 to 7, all different within a row; in each aligned block of 128 rows (0 to 127, 128 to 255, ...) at most 96 rows name the same one
- gate_weights: float32 [2048, 4], P(('dp', 'expert')), may hold values from 0.05 to 1
- proof_lengths: int32 [8], replicated, may hold values from 1 to 512, 2048 in all
- advantages: float32 [8], replicated, may hold values from -4 to 4
- hidden: bfloat16 [12288, 2880], P(('dp', 'expert'), 'tensor'), may hold values from -6 to 6
- down_weight: bfloat16 [8, 2880, 2880], P('expert', 'tensor'), may hold values from -0.109375 to 0.109375
Outputs:
- hidden_grad: bfloat16 [12288, 2880], P(('dp', 'expert'), 'tensor')
- down_grad: bfloat16 [8, 2880, 2880], P('expert', 'tensor', 'dp')
The draws below stay inside these ranges and needn't reach their ends.
Inputs may be any that keep to these rules, and one draw needn't show every extreme that they name: `expert_ids`: in each aligned block of 128 rows no expert is named by more than 96 rows, a bound that some block reaches. `proof_lengths`: the lengths sum to 2048; rollouts lie end to end in token order, and the longest has exactly 512 tokens.
All inputs are finite; a program needn't handle non-finite values.
Results may differ from the reference program's by a relative error of at most 0.0059.
Values may be sent and summed in bfloat16 or wider, within the bound.
A program may use at most 64 MiB of HBM per device.

```python
import math
import jax
import jax.numpy as jnp
import numpy as np
from jax import lax

D = 2880
FF = 2880
TOP = 4
TOK_DEV = 128
EXPERTS = 8
TOKENS = 2048
ROLLOUTS = 8
LONGEST = 512
CAP = 96
SLOTS = 768
ROWS = 12288
N_DP = 2
N_EXPERT = 8


def steps_of(stream_key, dims, pieces, least, top_value):
    loudness, own = 1.0, jax.random.fold_in(stream_key, 6)
    for axis_at, blocks in pieces:
        heights = jnp.exp(jax.random.uniform(jax.random.fold_in(own, axis_at), (blocks,), jnp.float32, least / len(pieces), top_value / len(pieces)))
        loudness = loudness * jnp.repeat(heights, dims[axis_at] // blocks).reshape([-1 if axis == axis_at else 1 for axis in range(len(dims))])
    return loudness


def split_up(count, total, bound, skew):
    weights = [(1 << 20) // math.isqrt(rank ** skew) + 1 for rank in range(2, count + 1)]
    surplus, counts = total - bound - (count - 1), [1] * (count - 1)
    while surplus > 0:
        free = [i for i in range(count - 1) if counts[i] < bound]
        mass, left = sum([weights[i] for i in free]), surplus
        for i in free:
            addition = min(bound - counts[i], max(1, left * weights[i] // mass), surplus)
            counts[i] = counts[i] + addition
            surplus = surplus - addition
    return np.array([bound] + counts)


def uneven_parts(key, number_of, total, bound, lean):
    if number_of == 2:
        one = jax.random.randint(key, (), max(1, total - bound), min(bound, total - 1) + 1)
        return jnp.stack([one, total - one])
    lengths = jnp.asarray(split_up(number_of, total, bound, lean), jnp.int32)
    couples = (number_of - 1) // 2
    source_of, sink = lengths[1:1 + 2 * couples:2], lengths[2:2 + 2 * couples:2]
    slack = jnp.minimum(source_of - 1, bound - sink)
    shifted = jax.random.randint(jax.random.fold_in(key, 1), (couples,), 0, 1 << 20) % (slack + 1)
    lengths = lengths.at[1:1 + 2 * couples:2].set(source_of - shifted).at[2:2 + 2 * couples:2].set(sink + shifted)
    return lengths[jax.random.permutation(jax.random.fold_in(key, 2), number_of)]


def shared_out(key, own, number, rows, count, top, limit, skew):
    ranking = jax.random.permutation(key, count)
    heavy_load, common = portions_of(count, rows * top, limit, skew, True), portions_of(count, rows * top, limit, skew, False)
    places = jnp.arange(count)

    def named(tallies, rotation):
        used = int((tallies > 0).sum())
        fixed = max(1, used // 4)
        passed = fixed + (places - fixed + rotation * (used - fixed)) % max(1, count - fixed)
        return jnp.zeros((count,), jnp.int32).at[ranking[jnp.where(places < fixed, places, passed)]].set(jnp.asarray(tallies, jnp.int32))

    tallies = jnp.where(number % 4 == 0, named(heavy_load, number // 4), named(common, number - number // 4 - 1))
    mixed = jax.random.permutation(jax.random.fold_in(own, 3), count)
    source_of, taker = mixed[0:count // 2 * 2:2], mixed[1:count // 2 * 2:2]
    room = jnp.minimum(tallies[source_of] - 1, limit - tallies[taker]) // 2
    room = jnp.where((source_of == ranking[0]) | (taker == ranking[0]) | (tallies[taker] == 0), 0, jnp.maximum(room, 0))
    passed = jax.random.randint(jax.random.fold_in(own, 4), (count // 2,), 0, 1 << 20) % (room + 1)
    tallies = tallies.at[source_of].add(-passed).at[taker].add(passed)
    labels = jnp.searchsorted(jnp.cumsum(tallies), jnp.arange(rows * top), side="right").astype(jnp.int32)
    table = labels.reshape(top, rows).T
    table = table[jax.random.permutation(jax.random.fold_in(own, 1), rows)]
    rotation = jax.random.randint(jax.random.fold_in(own, 2), (rows, 1), 0, top)
    return jnp.take_along_axis(table, (jnp.arange(top)[None, :] + rotation) % top, axis=1)


def portions_of(count, total, most, skew, full):
    weights = [(1 << 20) // math.isqrt(grade ** skew) + 1 for grade in range(1, count + 1)]
    largest = most if full else min(most, max(-(-total // count), total * weights[0] // sum(weights)))
    least = 1 if total - largest >= count - 1 else 0
    counts, rest = [largest] + [least] * (count - 1), total - largest - least * (count - 1)
    while rest > 0:
        movable = [i for i in range(1, count) if counts[i] < largest] or [i for i in range(1, count) if counts[i] < most]
        pool, budget = sum([weights[i] for i in movable]), rest
        for i in movable:
            extra = min(most - counts[i], max(1, budget * weights[i] // pool), rest)
            counts[i] = counts[i] + extra
            rest = rest - extra
    return np.array(counts)


def centred(stream_key, shape, width, most, shards=(), kind=jnp.bfloat16):
    array = width * jax.random.normal(stream_key, shape, jnp.float32)
    if shards:
        array = array * steps_of(stream_key, shape, shards, -0.22, 0.18)
    return jnp.clip(array, -most, most).astype(kind)


def setup_inputs(seed: int = 0) -> dict:
    streams_of = jax.random.split(jax.random.key(seed), 8)
    upstream = centred(streams_of[0], (TOKENS, D), 0.5, 3.0, ((0, 16), (1, 2)))
    expert_ids_keys = jax.random.split(jax.random.fold_in(streams_of[1], 1), TOKENS // TOK_DEV)
    expert_ids_turns = jax.random.permutation(jax.random.fold_in(streams_of[1], 3), TOKENS // TOK_DEV)
    expert_ids = jax.vmap(lambda own, number: shared_out(jax.random.fold_in(streams_of[1], 2), own, number, TOK_DEV, EXPERTS, TOP, CAP, 2))(expert_ids_keys, expert_ids_turns).reshape((TOKENS, TOP))
    gate_weights = jnp.clip(jnp.exp(math.log(1.0) - 2.9957323 * jax.random.uniform(streams_of[2], (TOKENS, TOP), jnp.float32) ** steps_of(streams_of[2], (TOKENS, TOP), ((0, 16),), -0.2, 0.2)), 0.05, 1.0)
    proof_lengths = uneven_parts(streams_of[3], ROLLOUTS, TOKENS, LONGEST, 2).astype(jnp.int32)
    advantages = centred(streams_of[4], (ROLLOUTS,), 1.0, 4.0, (), jnp.float32)
    hidden = centred(streams_of[5], (ROWS, FF), 1.0, 6.0, ((0, 16), (1, 2)))
    down_weight = centred(streams_of[6], (EXPERTS, FF, D), FF ** -0.5, 0.109375, ((0, 8), (1, 2)))
    return {"upstream": upstream, "expert_ids": expert_ids, "gate_weights": gate_weights, "proof_lengths": proof_lengths, "advantages": advantages, "hidden": hidden, "down_weight": down_weight}


def reference(upstream, expert_ids, gate_weights, proof_lengths, advantages, hidden, down_weight):
    positions = jnp.arange(TOKENS, dtype=jnp.int32)
    rollout_ends = jnp.cumsum(proof_lengths).astype(jnp.int32)
    rollout_of = jnp.sum((positions[:, None] >= rollout_ends[None, :]).astype(jnp.int32), axis=1)
    rollout_ids = jnp.arange(ROLLOUTS, dtype=jnp.int32)
    token_weight = jnp.sum(jnp.where(rollout_of[:, None] == rollout_ids[None, :], advantages[None, :], jnp.zeros((), advantages.dtype)), axis=1)
    scaled = ((token_weight[:, None] * gate_weights)[:, :, None] * upstream.astype(jnp.float32)[:, None, :]).astype(jnp.bfloat16)
    scaled = scaled.reshape(TOKENS * TOP, D)
    blocks = expert_ids.reshape(N_DP * N_EXPERT, TOK_DEV * TOP)
    onehot = (blocks[:, :, None] == jnp.arange(EXPERTS, dtype=jnp.int32)[None, None, :]).astype(jnp.int32)
    slot_index = jnp.sum((jnp.cumsum(onehot, axis=1) - onehot) * onehot, axis=2)
    block_index = jnp.arange(N_DP * N_EXPERT, dtype=jnp.int32)[:, None]
    replica_of = block_index // N_EXPERT
    source = block_index % N_EXPERT
    row_index = ((replica_of * EXPERTS + blocks) * SLOTS + source * CAP + slot_index).reshape(-1).astype(jnp.int32)
    slot_table = jnp.full((ROWS,), -1, jnp.int32).at[row_index].set(jnp.arange(TOKENS * TOP, dtype=jnp.int32))

    def per_expert(expert):
        weight = down_weight[expert]
        weight_total = jnp.zeros((FF, D), jnp.float32)
        grad_list = []
        for replica in range(N_DP):
            first_row = ((replica * EXPERTS + expert) * SLOTS).astype(jnp.int32)
            filled = lax.dynamic_slice_in_dim(slot_table, first_row, SLOTS, 0)
            routed_rows = jnp.where(filled[:, None] >= 0, scaled[jnp.maximum(filled, 0)], jnp.zeros((), scaled.dtype))
            activations = lax.dynamic_slice_in_dim(hidden, first_row, SLOTS, 0)
            grad_rows = lax.dot_general(routed_rows, weight, (((1,), (1,)), ((), ())), preferred_element_type=jnp.float32)
            grad_list.append(grad_rows.astype(jnp.bfloat16))
            half_term = lax.dot_general(activations, routed_rows, (((0,), (0,)), ((), ())), preferred_element_type=jnp.float32)
            half_term = lax.optimization_barrier(half_term.astype(jnp.bfloat16))
            weight_total = weight_total + half_term.astype(jnp.float32)
        return jnp.stack(grad_list), weight_total.astype(jnp.bfloat16)

    grad_groups, down_grad = lax.map(per_expert, jnp.arange(EXPERTS, dtype=jnp.int32))
    hidden_grad = jnp.transpose(grad_groups, (1, 0, 2, 3)).reshape(ROWS, FF)
    return hidden_grad, down_grad
```

```python
import functools

import jax
import jax.numpy as jnp
from jax import lax
from jax.experimental import pallas as pl
from jax.experimental.pallas import tpu as pltpu
from jax.sharding import PartitionSpec as P

MESH = pl.DeviceIdType.MESH
ROW_PAIR = 2


def from_partner(x, axis, stride):
    return lax.ppermute(x, axis, [(i, i ^ 1 << stride) for i in range(lax.axis_size(axis))])


def rows_times_weight(routed_rows, weight_cols):
    return lax.dot_general(
        routed_rows, weight_cols, (((1,), (1,)), ((), ())), preferred_element_type=jnp.float32
    )


def outer_sum(activations, routed_rows):
    return lax.dot_general(
        activations, routed_rows, (((0,), (0,)), ((), ())), preferred_element_type=jnp.float32
    )


def rounded_half(term):
    return lax.optimization_barrier(term.astype(jnp.bfloat16)).astype(jnp.float32)


def plain_local(upstream, expert_ids, gate_weights, proof_lengths, advantages, hidden, down_weight):
    experts = lax.axis_size("expert")
    tok_rows = upstream.shape[0]
    top_count = expert_ids.shape[1]
    slot_rows = hidden.shape[0]
    capacity = slot_rows // experts
    block_index = lax.axis_index("dp") * experts + lax.axis_index("expert")
    positions = block_index * tok_rows + lax.iota(jnp.int32, tok_rows)
    rollout_ends = jnp.cumsum(proof_lengths)
    rollout_of = jnp.sum((positions[:, None] >= rollout_ends[None, :]).astype(jnp.int32), axis=1)
    rollout_ids = lax.iota(jnp.int32, rollout_ends.shape[0])
    token_weight = jnp.sum(
        jnp.where(
            rollout_of[:, None] == rollout_ids[None, :],
            advantages[None, :],
            jnp.zeros((), advantages.dtype),
        ),
        axis=1,
    )
    scaled = (
        (token_weight[:, None] * gate_weights)[:, :, None]
        * upstream.astype(jnp.float32)[:, None, :]
    ).astype(jnp.bfloat16)
    scaled = scaled.reshape(tok_rows * top_count, upstream.shape[1])
    flat_ids = expert_ids.reshape(-1)
    onehot = (flat_ids[:, None] == lax.iota(jnp.int32, experts)[None, :]).astype(jnp.int32)
    slot_index = jnp.sum((jnp.cumsum(onehot, axis=0) - onehot) * onehot, axis=1)
    target = flat_ids * capacity + slot_index
    outgoing = (
        jnp.zeros((experts * capacity, upstream.shape[1]), jnp.bfloat16).at[target].set(scaled)
    )
    arrived = lax.all_to_all(outgoing, "expert", split_axis=0, concat_axis=0, tiled=True)
    w_local = down_weight[0]
    model_cols = w_local.shape[1]
    routed = lax.all_gather(arrived, "tensor", axis=1, tiled=True)
    grad_hidden = rows_times_weight(routed, w_local)
    half_cols = model_cols // 2
    own_index = lax.axis_index("dp")
    partner_cols = lax.dynamic_slice_in_dim(routed, (1 - own_index) * half_cols, half_cols, 1)
    partner_rows, partner_hidden = from_partner((partner_cols, hidden), "dp", 0)
    own_cols = lax.dynamic_slice_in_dim(routed, own_index * half_cols, half_cols, 1)
    grad_shard = rounded_half(outer_sum(hidden, own_cols)) + rounded_half(
        outer_sum(partner_hidden, partner_rows)
    )
    return (grad_hidden.astype(jnp.bfloat16), grad_shard.astype(jnp.bfloat16)[None])


def fast_kernel(
    n_z, capacity, up, hid_in, w_in, meta_in, hg_out, dg_out,
    tok, oth, hidp, hid, w, acc, hgbuf, dgbuf, routed, meta,
    z_send, z_recv, y_send, y_recv, c_send, c_recv, x_send, x_recv, h_send, h_recv,
    m_send, m_recv, load_sem, store_sem,
):
    d, e, t = lax.axis_index("dp"), lax.axis_index("expert"), lax.axis_index("tensor")
    n_e = n_z * ROW_PAIR
    z, y = e // ROW_PAIR, e % ROW_PAIR
    n_peer = 2 * n_e
    me = d * n_e + e
    tok_rows, cols = up.shape
    half = tok_rows // 2
    pair_rows = ROW_PAIR * capacity
    od, ot, ey = 1 - d, 1 - t, z * ROW_PAIR + 1 - y

    barrier = pltpu.get_barrier_semaphore()

    def greet(k, _):
        peer = (me + k) % n_peer
        pl.semaphore_signal(
            barrier, inc=1, device_id={"dp": peer // n_e, "expert": peer % n_e}, device_id_type=MESH
        )
        return 0

    lax.fori_loop(1, n_peer, greet, 0)
    pl.semaphore_signal(barrier, inc=1, device_id={"tensor": ot}, device_id_type=MESH)
    pl.semaphore_signal(
        barrier, inc=1, device_id={"dp": od, "tensor": ot}, device_id_type=MESH
    )

    loads = [
        pltpu.make_async_copy(up, tok.at[e, t], load_sem.at[0]),
        pltpu.make_async_copy(meta_in.at[e], meta.at[me], load_sem.at[1]),
        pltpu.make_async_copy(w_in, w, load_sem.at[2]),
        pltpu.make_async_copy(hid_in, hid, load_sem.at[3]),
    ]
    for load in loads:
        load.start()
    pl.semaphore_wait(barrier, n_peer + 1)

    def send(src, dst, ss, rs, where):
        return pltpu.make_async_remote_copy(
            src_ref=src, dst_ref=dst, send_sem=ss, recv_sem=rs, device_id=where, device_id_type=MESH
        )

    def x_copy(part):
        rows = pl.ds(part * half, half)
        return send(
            up.at[rows], oth.at[e, rows], x_send.at[part], x_recv.at[0], {"dp": od, "tensor": jnp.int32(part)}
        )

    @pl.when(t == od)
    def _():
        x_copy(0).start()
        x_copy(1).start()

    def m_copy(k):
        peer = (me + k) % n_peer
        return send(
            meta_in.at[peer % n_e], meta.at[me], m_send.at[k], m_recv.at[k],
            {"dp": peer // n_e, "expert": peer % n_e},
        )

    def m_start(k, _):
        m_copy(k).start()
        return 0

    def slab(part, b):
        if part == 0:
            return tok.at[b, t]
        return oth.at[b, pl.ds(pl.multiple_of(t * half, half), half)]

    def z_copy(part, zz, delta, own=False):
        b = zz * ROW_PAIR + y
        src = up if own and part == 0 else slab(part, b)
        return send(
            src, slab(part, b), z_send.at[part, (delta + 1) // 2, zz], z_recv.at[part, zz],
            {"expert": (z + delta) * ROW_PAIR + y},
        )

    def y_copy(part, zz, own=False):
        b = zz * ROW_PAIR + y
        src = up if own and part == 0 else slab(part, b)
        return send(src, slab(part, b), y_send.at[part, zz], y_recv.at[part, zz], {"expert": ey})

    def y_arrival(part, zz):
        b = zz * ROW_PAIR + 1 - y
        return send(slab(part, b), slab(part, b), y_send.at[part, zz], y_recv.at[part, zz], {"expert": ey})

    def c_copy(part, b, own=False):
        src = up if own and part == 0 else slab(part, b)
        return send(src, slab(part, b), c_send.at[part, b], c_recv.at[part, b], {"tensor": ot})

    def c_arrival(part, b):
        if part == 0:
            dst = tok.at[b, ot]
        else:
            dst = oth.at[b, pl.ds(pl.multiple_of(ot * half, half), half)]
        return send(dst, dst, c_send.at[part, b], c_recv.at[part, b], {"tensor": ot})

    def pair_of(i):
        zz, bit = 0, 1
        while bit < n_z:
            zz = zz + (((z // bit) % 2 + (i // bit) % 2) % 2) * bit
            bit *= 2
        return zz

    def pair_slice(zz):
        return pl.ds(pl.multiple_of(zz * pair_rows, pair_rows), pair_rows)

    def h_copy(i):
        rows = pair_slice(pair_of(i))
        return send(hid_in.at[rows], hidp.at[rows], h_send.at[i], h_recv.at[i], {"dp": od})

    def spread(part):
        y_copy(part, z, True).start()
        for delta in (1, -1):
            @pl.when((z + delta >= 0) & (z + delta < n_z))
            def _():
                z_copy(part, z, delta, True).start()
        c_copy(part, e, True).start()

    lax.fori_loop(1, n_peer, m_start, 0)
    spread(0)

    def h_start(i, _):
        h_copy(i).start()
        return 0

    lax.fori_loop(0, n_z, h_start, 0)
    x_in = send(
        slab(1, e), slab(1, e), x_send.at[0], x_recv.at[0], {"dp": od}
    )
    x_in.wait_recv()
    spread(1)

    acc[...] = jnp.zeros_like(acc)
    for load in loads:
        load.wait()

    def m_land(k, _):
        frm = (me + n_peer - k) % n_peer
        send(
            meta.at[frm], meta.at[frm], m_send.at[k], m_recv.at[k],
            {"dp": frm // n_e, "expert": frm % n_e},
        ).wait_recv()
        return 0

    lax.fori_loop(1, n_peer, m_land, 0)

    def place(tokens, info):
        slots, scale = info[0:1, :], info[1:2, :]
        at = lax.broadcasted_iota(jnp.int32, (capacity, tok_rows), 0).astype(jnp.float32)
        hit = at == slots
        row_scale = jnp.sum(jnp.where(hit, scale, 0.0), axis=1, keepdims=True)
        pick = jnp.where(hit, 1.0, 0.0).astype(jnp.bfloat16)
        return jnp.dot(pick, tokens, preferred_element_type=jnp.float32) * row_scale

    col_tiles = [(c, min(384, cols - c)) for c in range(0, cols, 384)]

    def compute(i):
        zz = pair_of(i)
        rows = pair_slice(zz)
        for k in range(ROW_PAIR):
            b = zz * ROW_PAIR + k
            to = slice(k * capacity, (k + 1) * capacity)
            info = meta[d * n_e + b]
            r0, r1 = place(tok[b, 0], info), place(tok[b, 1], info)
            routed[0, to, :] = jnp.concatenate([r0, r1], axis=1).astype(jnp.bfloat16)
            routed[1, to, :cols] = jnp.where(d == 0, r0, r1).astype(jnp.bfloat16)
            other = place(oth[b], meta[od * n_e + b])
            routed[2, to, :cols] = other.astype(jnp.bfloat16)
        for c, n in col_tiles:
            hgbuf[rows, c:c + n] = lax.dot_general(
                routed[0], w[c:c + n, :], (((1,), (1,)), ((), ())), preferred_element_type=jnp.float32
            ).astype(jnp.bfloat16)
        pltpu.make_async_copy(hgbuf.at[rows], hg_out.at[rows], store_sem.at[i]).start()
        send(hidp.at[rows], hidp.at[rows], h_send.at[i], h_recv.at[i], {"dp": od}).wait_recv()
        for c, n in col_tiles:
            own = lax.dot_general(
                hid[rows, c:c + n], routed[1, :, :cols], (((0,), (0,)), ((), ())),
                preferred_element_type=jnp.float32,
            )
            partner = lax.dot_general(
                hidp[rows, c:c + n], routed[2, :, :cols], (((0,), (0,)), ((), ())),
                preferred_element_type=jnp.float32,
            )
            acc[c:c + n, :] += own + partner

    def step(s, _):
        for k in (0, 1):
            delta = (1 - 2 * (z % 2)) * (1 - 2 * k)
            zz = z + delta * s

            @pl.when((s < n_z) & (zz >= 0) & (zz < n_z))
            def _():
                for part in (0, 1):
                    b = zz * ROW_PAIR + y
                    send(
                        slab(part, b), slab(part, b), z_send.at[part, 0, zz], z_recv.at[part, zz],
                        {"expert": ey},
                    ).wait_recv()

                    @pl.when((z - delta >= 0) & (z - delta < n_z))
                    def _():
                        z_copy(part, zz, -delta).start()

                    y_copy(part, zz).start()
                    c_copy(part, b).start()

        @pl.when(s <= n_z)
        def _():
            zz = pair_of(s - 1)
            for part in (0, 1):
                y_arrival(part, zz).wait_recv()
                c_copy(part, zz * ROW_PAIR + 1 - y).start()

        @pl.when(s >= 2)
        def _():
            zz = pair_of(s - 2)
            for k in range(ROW_PAIR):
                for part in (0, 1):
                    c_arrival(part, zz * ROW_PAIR + k).wait_recv()
            compute(s - 2)
        return 0

    lax.fori_loop(1, n_z + 2, step, 0)

    dgbuf[...] = acc[...].astype(jnp.bfloat16)
    out = pltpu.make_async_copy(dgbuf, dg_out, load_sem.at[0])
    out.start()

    @pl.when(t == od)
    def _():
        x_copy(0).wait_send()
        x_copy(1).wait_send()

    def m_sent(k, _):
        m_copy(k).wait_send()
        return 0

    lax.fori_loop(1, n_peer, m_sent, 0)

    def sent(zz, _):
        for part in (0, 1):
            y_copy(part, zz).wait_send()
            for k in range(ROW_PAIR):
                c_copy(part, zz * ROW_PAIR + k).wait_send()
            for delta in (1, -1):
                @pl.when((z + delta >= 0) & (z + delta < n_z) & ((z - zz) * delta >= 0))
                def _():
                    z_copy(part, zz, delta).wait_send()
        h_copy(zz).wait_send()
        rows = pair_slice(pair_of(zz))
        pltpu.make_async_copy(hgbuf.at[rows], hg_out.at[rows], store_sem.at[zz]).wait()
        return 0

    lax.fori_loop(0, n_z, sent, 0)
    out.wait()


def fast_local(upstream, expert_ids, gate_weights, proof_lengths, advantages, hidden, down_weight):
    n_e = lax.axis_size("expert")
    n_z = n_e // ROW_PAIR
    tok_rows, cols = upstream.shape
    slot_rows, units = hidden.shape
    capacity = slot_rows // n_e
    model = down_weight.shape[2]
    block_index = lax.axis_index("dp") * n_e + lax.axis_index("expert")
    positions = block_index * tok_rows + lax.iota(jnp.int32, tok_rows)
    rollouts = proof_lengths.shape[0]
    ids = lax.iota(jnp.int32, rollouts)
    rollout_ends = jnp.sum(jnp.where(ids[:, None] <= ids[None, :], proof_lengths[:, None], 0), axis=0)
    rollout_of = jnp.sum((positions[:, None] >= rollout_ends[None, :]).astype(jnp.int32), axis=1)
    token_weight = jnp.sum(
        jnp.where(rollout_of[:, None] == ids[None, :], advantages[None, :], 0.0), axis=1
    )
    scale = token_weight[:, None] * gate_weights
    named = expert_ids[None, :, :] == lax.iota(jnp.int32, n_e)[:, None, None]
    member = jnp.any(named, axis=2)
    scale_of = jnp.sum(jnp.where(named, scale[None], 0.0), axis=2)
    order = lax.iota(jnp.int32, tok_rows)
    before = jnp.sum(
        (member[:, :, None] & (order[:, None] < order[None, :])[None]).astype(jnp.float32), axis=1
    )
    slot = jnp.where(member, before, -1.0)
    meta = jnp.pad(jnp.stack([slot, scale_of], axis=1), ((0, 0), (0, 6), (0, 0)))
    dma = pltpu.SemaphoreType.DMA
    bf16 = jnp.bfloat16
    hg, dg = pl.pallas_call(
        functools.partial(fast_kernel, n_z, capacity),
        out_shape=(
            jax.ShapeDtypeStruct((slot_rows, units), bf16),
            jax.ShapeDtypeStruct((units, cols), bf16),
        ),
        in_specs=[pl.BlockSpec(memory_space=pl.ANY)] * 4,
        out_specs=(pl.BlockSpec(memory_space=pl.ANY),) * 2,
        scratch_shapes=[
            pltpu.VMEM((n_e, 2, tok_rows, cols), bf16),
            pltpu.VMEM((n_e, tok_rows, cols), bf16),
            pltpu.VMEM((slot_rows, units), bf16),
            pltpu.VMEM((slot_rows, units), bf16),
            pltpu.VMEM((units, model), bf16),
            pltpu.VMEM((units, cols), jnp.float32),
            pltpu.VMEM((slot_rows, units), bf16),
            pltpu.VMEM((units, cols), bf16),
            pltpu.VMEM((3, ROW_PAIR * capacity, model), bf16),
            pltpu.VMEM((2 * n_e, 8, tok_rows), jnp.float32),
            dma((2, 2, n_z)), dma((2, n_z)), dma((2, n_z)), dma((2, n_z)),
            dma((2, n_e)), dma((2, n_e)), dma((2,)), dma((1,)), dma((n_z,)), dma((n_z,)),
            dma((2 * n_e,)), dma((2 * n_e,)), dma((4,)), dma((n_z,)),
        ],
        compiler_params=pltpu.CompilerParams(
            collective_id=0, has_side_effects=True, vmem_limit_bytes=60000 * 1024
        ),
    )(upstream, hidden, down_weight[0], meta)
    return hg, dg[None]


def fits_fast(mesh):
    n_e = mesh.shape["expert"]
    return mesh.shape["dp"] == 2 and mesh.shape["tensor"] == 2 and n_e in (4, 8, 16)


def solution(mesh):
    return jax.shard_map(
        fast_local if fits_fast(mesh) else plain_local,
        mesh=mesh,
        in_specs=(
            P(("dp", "expert"), "tensor"),
            P(("dp", "expert"), None),
            P(("dp", "expert"), None),
            P(),
            P(),
            P(("dp", "expert"), "tensor"),
            P("expert", "tensor", None),
        ),
        out_specs=(P(("dp", "expert"), "tensor"), P("expert", "tensor", "dp")),
        check_vma=False,
    )
```

```python
import functools

import jax
import jax.numpy as jnp
from jax import lax
from jax.experimental import pallas as pl
from jax.experimental.pallas import tpu as pltpu
from jax.sharding import PartitionSpec as P

MESH = pl.DeviceIdType.MESH
ROW_PAIR = 2


def from_partner(x, axis, stride):
    return lax.ppermute(x, axis, [(i, i ^ 1 << stride) for i in range(lax.axis_size(axis))])


def rows_times_weight(routed_rows, weight_cols):
    return lax.dot_general(
        routed_rows, weight_cols, (((1,), (1,)), ((), ())), preferred_element_type=jnp.float32
    )


def outer_sum(activations, routed_rows):
    return lax.dot_general(
        activations, routed_rows, (((0,), (0,)), ((), ())), preferred_element_type=jnp.float32
    )


def rounded_half(term):
    return lax.optimization_barrier(term.astype(jnp.bfloat16)).astype(jnp.float32)


def plain_local(upstream, expert_ids, gate_weights, proof_lengths, advantages, hidden, down_weight):
    experts = lax.axis_size("expert")
    tok_rows = upstream.shape[0]
    top_count = expert_ids.shape[1]
    slot_rows = hidden.shape[0]
    capacity = slot_rows // experts
    block_index = lax.axis_index("dp") * experts + lax.axis_index("expert")
    positions = block_index * tok_rows + lax.iota(jnp.int32, tok_rows)
    rollout_ends = jnp.cumsum(proof_lengths)
    rollout_of = jnp.sum((positions[:, None] >= rollout_ends[None, :]).astype(jnp.int32), axis=1)
    rollout_ids = lax.iota(jnp.int32, rollout_ends.shape[0])
    token_weight = jnp.sum(
        jnp.where(
            rollout_of[:, None] == rollout_ids[None, :],
            advantages[None, :],
            jnp.zeros((), advantages.dtype),
        ),
        axis=1,
    )
    scaled = (
        (token_weight[:, None] * gate_weights)[:, :, None]
        * upstream.astype(jnp.float32)[:, None, :]
    ).astype(jnp.bfloat16)
    scaled = scaled.reshape(tok_rows * top_count, upstream.shape[1])
    flat_ids = expert_ids.reshape(-1)
    onehot = (flat_ids[:, None] == lax.iota(jnp.int32, experts)[None, :]).astype(jnp.int32)
    slot_index = jnp.sum((jnp.cumsum(onehot, axis=0) - onehot) * onehot, axis=1)
    target = flat_ids * capacity + slot_index
    outgoing = (
        jnp.zeros((experts * capacity, upstream.shape[1]), jnp.bfloat16).at[target].set(scaled)
    )
    arrived = lax.all_to_all(outgoing, "expert", split_axis=0, concat_axis=0, tiled=True)
    w_local = down_weight[0]
    model_cols = w_local.shape[1]
    routed = lax.all_gather(arrived, "tensor", axis=1, tiled=True)
    grad_hidden = rows_times_weight(routed, w_local)
    half_cols = model_cols // 2
    own_index = lax.axis_index("dp")
    partner_cols = lax.dynamic_slice_in_dim(routed, (1 - own_index) * half_cols, half_cols, 1)
    partner_rows, partner_hidden = from_partner((partner_cols, hidden), "dp", 0)
    own_cols = lax.dynamic_slice_in_dim(routed, own_index * half_cols, half_cols, 1)
    grad_shard = rounded_half(outer_sum(hidden, own_cols)) + rounded_half(
        outer_sum(partner_hidden, partner_rows)
    )
    return (grad_hidden.astype(jnp.bfloat16), grad_shard.astype(jnp.bfloat16)[None])


def fast_kernel(
    n_z, capacity, up, hid_in, w_in, ids_in, gate_in, lengths, advantages, hg_out, dg_out,
    tok, oth, hidp, hid, w, acc, hgbuf, dgbuf, routed, own_routed, ids, gates, info,
    z_send, z_recv, y_send, y_recv, c_send, c_recv, x_send, x_recv, h_send, h_recv,
    m_send, m_recv, g_send, g_recv, load_sem, store_sem,
):
    d, e, t = lax.axis_index("dp"), lax.axis_index("expert"), lax.axis_index("tensor")
    n_e = n_z * ROW_PAIR
    z, y = e // ROW_PAIR, e % ROW_PAIR
    n_peer = 2 * n_e
    me = d * n_e + e
    cols, tok_rows = up.shape
    half = cols // 2
    couple = 2 * ROW_PAIR * capacity
    lane = couple // 3
    window = 2 * lane
    top = ids_in.shape[0]
    od, ot, ey = 1 - d, 1 - t, z * ROW_PAIR + 1 - y

    barrier = pltpu.get_barrier_semaphore()

    def greet(k, _):
        peer = (me + k) % n_peer
        pl.semaphore_signal(
            barrier, inc=1, device_id={"dp": peer // n_e, "expert": peer % n_e}, device_id_type=MESH
        )
        return 0

    lax.fori_loop(1, n_peer, greet, 0)
    pl.semaphore_signal(barrier, inc=1, device_id={"tensor": ot}, device_id_type=MESH)
    pl.semaphore_signal(
        barrier, inc=1, device_id={"dp": od, "tensor": ot}, device_id_type=MESH
    )

    loads = [
        pltpu.make_async_copy(up, tok.at[e, t], load_sem.at[0]),
        pltpu.make_async_copy(ids_in, ids.at[me], load_sem.at[1]),
        pltpu.make_async_copy(gate_in, gates.at[me], load_sem.at[4]),
        pltpu.make_async_copy(w_in, w, load_sem.at[2]),
        pltpu.make_async_copy(hid_in, hid, load_sem.at[3]),
    ]
    for load in loads:
        load.start()
    pl.semaphore_wait(barrier, n_peer + 1)

    def send(src, dst, ss, rs, where):
        return pltpu.make_async_remote_copy(
            src_ref=src, dst_ref=dst, send_sem=ss, recv_sem=rs, device_id=where, device_id_type=MESH
        )

    def x_copy(part):
        rows = pl.ds(part * half, half)
        return send(
            up.at[rows], oth.at[e, rows], x_send.at[part], x_recv.at[0], {"dp": od, "tensor": jnp.int32(part)}
        )

    @pl.when(t == od)
    def _():
        x_copy(0).start()
        x_copy(1).start()

    def m_copies(k, frm):
        peer = (me + k) % n_peer
        where = {"dp": peer // n_e, "expert": peer % n_e}
        return (
            send(ids_in, ids.at[frm], m_send.at[k], m_recv.at[k], where),
            send(gate_in, gates.at[frm], g_send.at[k], g_recv.at[k], where),
        )

    def m_start(k, _):
        for copy in m_copies(k, me):
            copy.start()
        return 0

    def slab(part, b):
        if part == 0:
            return tok.at[b, t]
        return oth.at[b, pl.ds(pl.multiple_of(t * half, half), half)]

    def z_copy(part, zz, delta, own=False):
        b = zz * ROW_PAIR + y
        src = up if own and part == 0 else slab(part, b)
        return send(
            src, slab(part, b), z_send.at[part, (delta + 1) // 2, zz], z_recv.at[part, zz],
            {"expert": (z + delta) * ROW_PAIR + y},
        )

    def y_copy(part, zz, own=False):
        b = zz * ROW_PAIR + y
        src = up if own and part == 0 else slab(part, b)
        return send(src, slab(part, b), y_send.at[part, zz], y_recv.at[part, zz], {"expert": ey})

    def y_arrival(part, zz):
        b = zz * ROW_PAIR + 1 - y
        return send(slab(part, b), slab(part, b), y_send.at[part, zz], y_recv.at[part, zz], {"expert": ey})

    def c_copy(part, b, own=False):
        src = up if own and part == 0 else slab(part, b)
        return send(src, slab(part, b), c_send.at[part, b], c_recv.at[part, b], {"tensor": ot})

    def c_arrival(part, b):
        if part == 0:
            dst = tok.at[b, ot]
        else:
            dst = oth.at[b, pl.ds(pl.multiple_of(ot * half, half), half)]
        return send(dst, dst, c_send.at[part, b], c_recv.at[part, b], {"tensor": ot})

    def pair_of(i):
        zz, bit = 0, 1
        while bit < n_z:
            zz = zz + (((z // bit) % 2 + (i // bit) % 2) % 2) * bit
            bit *= 2
        return zz

    def pair_window(zz):
        return pl.ds(pl.multiple_of((zz // 2) * couple + (zz % 2) * lane, lane), window)

    def h_lanes(i, size):
        zz = pair_of(i)
        at = (zz // 2) * couple + (zz % 2) * (lane if size == window else 2 * lane)
        return pl.ds(pl.multiple_of(at, lane), size)

    def h_copy(j, size):
        lanes = h_lanes(2 * j + (0 if size == window else 1), size)
        i = 2 * j + (0 if size == window else 1)
        return send(
            hid_in.at[:, lanes], hidp.at[:, lanes], h_send.at[i], h_recv.at[i], {"dp": od}
        )

    def spread(part):
        y_copy(part, z, True).start()
        for delta in (1, -1):
            @pl.when((z + delta >= 0) & (z + delta < n_z))
            def _():
                z_copy(part, z, delta, True).start()
        c_copy(part, e, True).start()

    lax.fori_loop(1, n_peer, m_start, 0)
    spread(0)

    def h_start(j, _):
        h_copy(j, window).start()
        h_copy(j, lane).start()
        return 0

    lax.fori_loop(0, n_z // 2, h_start, 0)
    x_in = send(
        slab(1, e), slab(1, e), x_send.at[0], x_recv.at[0], {"dp": od}
    )
    x_in.wait_recv()
    spread(1)

    acc[...] = jnp.zeros_like(acc)
    hgbuf[...] = jnp.zeros_like(hgbuf)
    for load in loads:
        load.wait()

    ends, end = [], 0
    for r in range(lengths.shape[0]):
        end = end + lengths[r]
        ends.append(end)
    order = lax.broadcasted_iota(jnp.int32, (tok_rows, tok_rows), 0)
    later = lax.broadcasted_iota(jnp.int32, (tok_rows, tok_rows), 1)
    earlier = jnp.where(order < later, 1.0, 0.0).astype(jnp.bfloat16)

    def m_land(k, _):
        frm = (me + n_peer - k) % n_peer

        @pl.when(k > 0)
        def _():
            for copy in m_copies(k, frm):
                copy.wait_recv()

        named = ids[frm] == e
        token = frm * tok_rows + lax.broadcasted_iota(jnp.int32, (top, tok_rows), 1)
        rollout = jnp.zeros((top, tok_rows), jnp.int32)
        for end in ends:
            rollout = rollout + (token >= end).astype(jnp.int32)
        weight = jnp.zeros((top, tok_rows), jnp.float32)
        for r in range(lengths.shape[0]):
            weight = weight + jnp.where(rollout == r, advantages[r], 0.0)
        scale = jnp.sum(jnp.where(named, weight * gates[frm], 0.0), axis=0, keepdims=True)
        member = jnp.sum(jnp.where(named, 1.0, 0.0), axis=0, keepdims=True)
        member = jnp.broadcast_to(member, (8, tok_rows))
        before = jnp.dot(member.astype(jnp.bfloat16), earlier, preferred_element_type=jnp.float32)
        slot = jnp.where(member > 0.5, before, -float(2 * couple))
        row = lax.broadcasted_iota(jnp.int32, (8, tok_rows), 0)
        both = jnp.where(row == 0, slot, jnp.broadcast_to(scale, (8, tok_rows)))
        info[frm] = jnp.transpose(both)
        return 0

    lax.fori_loop(0, n_peer, m_land, 0)

    row_tiles = [(c, min(480, cols - c)) for c in range(0, cols, 480)]

    def picks(half_index, zz):
        base = half_index * n_e + zz * ROW_PAIR
        at = lax.broadcasted_iota(jnp.int32, (tok_rows, window), 1)
        at = (at - (zz % 2) * (couple // 2 - lane)).astype(jnp.float32)
        pick, scale = [], 0.0
        for k in range(ROW_PAIR):
            block = info[base + k]
            hit = at - k * capacity == block[:, 0:1]
            scale = scale + jnp.sum(jnp.where(hit, block[:, 1:2], 0.0), axis=0, keepdims=True)
            pick.append(jnp.where(hit, 1.0, 0.0).astype(jnp.bfloat16))
        return jnp.concatenate(pick, axis=0), scale

    def compute(i):
        zz = pair_of(i)
        slots = pair_window(zz)
        b = zz * ROW_PAIR
        pick, scale = picks(d, zz)
        opick, oscale = picks(od, zz)
        for side in range(2):
            for c, n in row_tiles:
                tokens = jnp.concatenate([tok[b + k, side, c:c + n, :] for k in range(ROW_PAIR)], axis=1)
                rows = jnp.dot(tokens, pick, preferred_element_type=jnp.float32) * scale
                routed[side * cols + c:side * cols + c + n, :] = rows.astype(jnp.bfloat16)
        for c, n in row_tiles:
            tokens = jnp.concatenate([oth[b + k, c:c + n, :] for k in range(ROW_PAIR)], axis=1)
            rows = jnp.dot(tokens, opick, preferred_element_type=jnp.float32) * oscale
            own_routed[c:c + n, window:] = rows.astype(jnp.bfloat16)
        own_routed[:, :window] = routed[pl.ds(pl.multiple_of(d * cols, 16), cols), :]
        at = lax.broadcasted_iota(jnp.int32, (1, window), 1)
        start = (zz % 2) * (couple // 2 - lane)
        mine = (at >= start) & (at < start + couple // 2)
        for c, n in row_tiles:
            rows = jnp.dot(w[c:c + n, :], routed[...], preferred_element_type=jnp.float32)
            hgbuf[c:c + n, slots] = jnp.where(mine, rows, hgbuf[c:c + n, slots].astype(jnp.float32)).astype(jnp.bfloat16)

        @pl.when(i % 2 == 1)
        def _():
            hg_store(i // 2).start()

        for parity, size in ((0, window), (1, lane)):
            @pl.when(i % 2 == parity)
            def _():
                h_copy(i // 2, size).wait_recv()

        for c, n in row_tiles:
            left = jnp.concatenate([hid[c:c + n, slots], hidp[c:c + n, slots]], axis=1)
            acc[c:c + n, :] += lax.dot_general(
                left, own_routed[...], (((1,), (1,)), ((), ())), preferred_element_type=jnp.float32
            )

    def hg_store(j):
        lanes = pl.ds(pl.multiple_of((pair_of(2 * j) // 2) * couple, couple), couple)
        return pltpu.make_async_copy(hgbuf.at[:, lanes], hg_out.at[:, lanes], store_sem.at[j])

    def step(s, _):
        for k in (0, 1):
            delta = (1 - 2 * (z % 2)) * (1 - 2 * k)
            zz = z + delta * s

            @pl.when((s < n_z) & (zz >= 0) & (zz < n_z))
            def _():
                for part in (0, 1):
                    b = zz * ROW_PAIR + y
                    send(
                        slab(part, b), slab(part, b), z_send.at[part, 0, zz], z_recv.at[part, zz],
                        {"expert": ey},
                    ).wait_recv()

                    @pl.when((z - delta >= 0) & (z - delta < n_z))
                    def _():
                        z_copy(part, zz, -delta).start()

                    y_copy(part, zz).start()
                    c_copy(part, b).start()

        @pl.when(s <= n_z)
        def _():
            zz = pair_of(s - 1)
            for part in (0, 1):
                y_arrival(part, zz).wait_recv()
                c_copy(part, zz * ROW_PAIR + 1 - y).start()

        @pl.when(s >= 2)
        def _():
            zz = pair_of(s - 2)
            for k in range(ROW_PAIR):
                for part in (0, 1):
                    c_arrival(part, zz * ROW_PAIR + k).wait_recv()
            compute(s - 2)
        return 0

    lax.fori_loop(1, n_z + 2, step, 0)

    dgbuf[...] = acc[...].astype(jnp.bfloat16)
    out = pltpu.make_async_copy(dgbuf, dg_out, load_sem.at[0])
    out.start()

    @pl.when(t == od)
    def _():
        x_copy(0).wait_send()
        x_copy(1).wait_send()

    def m_sent(k, _):
        for copy in m_copies(k, me):
            copy.wait_send()
        return 0

    lax.fori_loop(1, n_peer, m_sent, 0)

    def sent(zz, _):
        for part in (0, 1):
            y_copy(part, zz).wait_send()
            for k in range(ROW_PAIR):
                c_copy(part, zz * ROW_PAIR + k).wait_send()
            for delta in (1, -1):
                @pl.when((z + delta >= 0) & (z + delta < n_z) & ((z - zz) * delta >= 0))
                def _():
                    z_copy(part, zz, delta).wait_send()
        return 0

    lax.fori_loop(0, n_z, sent, 0)

    def stored(j, _):
        h_copy(j, window).wait_send()
        h_copy(j, lane).wait_send()
        hg_store(j).wait()
        return 0

    lax.fori_loop(0, n_z // 2, stored, 0)
    out.wait()


def fast_local(upstream, expert_ids, gate_weights, proof_lengths, advantages, hidden, down_weight):
    n_e = lax.axis_size("expert")
    n_z = n_e // ROW_PAIR
    tok_rows, cols = upstream.shape
    slot_rows, units = hidden.shape
    capacity = slot_rows // n_e
    top = expert_ids.shape[1]
    window = 4 * ROW_PAIR * capacity // 3
    model = down_weight.shape[2]
    dma = pltpu.SemaphoreType.DMA
    bf16 = jnp.bfloat16
    hg, dg = pl.pallas_call(
        functools.partial(fast_kernel, n_z, capacity),
        out_shape=(
            jax.ShapeDtypeStruct((units, slot_rows), bf16),
            jax.ShapeDtypeStruct((units, cols), bf16),
        ),
        in_specs=[pl.BlockSpec(memory_space=pl.ANY)] * 5
        + [pl.BlockSpec(memory_space=pltpu.SMEM)] * 2,
        out_specs=(pl.BlockSpec(memory_space=pl.ANY),) * 2,
        scratch_shapes=[
            pltpu.VMEM((n_e, 2, cols, tok_rows), bf16),
            pltpu.VMEM((n_e, cols, tok_rows), bf16),
            pltpu.VMEM((units, slot_rows), bf16),
            pltpu.VMEM((units, slot_rows), bf16),
            pltpu.VMEM((units, model), bf16),
            pltpu.VMEM((units, cols), jnp.float32),
            pltpu.VMEM((units, slot_rows), bf16),
            pltpu.VMEM((units, cols), bf16),
            pltpu.VMEM((model, window), bf16),
            pltpu.VMEM((cols, 2 * window), bf16),
            pltpu.VMEM((2 * n_e, top, tok_rows), jnp.int32),
            pltpu.VMEM((2 * n_e, top, tok_rows), jnp.float32),
            pltpu.VMEM((2 * n_e, tok_rows, 8), jnp.float32),
            dma((2, 2, n_z)), dma((2, n_z)), dma((2, n_z)), dma((2, n_z)),
            dma((2, n_e)), dma((2, n_e)), dma((2,)), dma((1,)), dma((n_z,)), dma((n_z,)),
            dma((2 * n_e,)), dma((2 * n_e,)), dma((2 * n_e,)), dma((2 * n_e,)), dma((5,)), dma((n_z // 2,)),
        ],
        compiler_params=pltpu.CompilerParams(
            collective_id=0, has_side_effects=True, vmem_limit_bytes=60000 * 1024
        ),
    )(
        upstream.T, hidden.T, down_weight[0], expert_ids.T, gate_weights.T, proof_lengths, advantages
    )
    return hg.T, dg[None]


def fits_fast(mesh):
    n_e = mesh.shape["expert"]
    return mesh.shape["dp"] == 2 and mesh.shape["tensor"] == 2 and n_e in (4, 8, 16)


def solution(mesh):
    return jax.shard_map(
        fast_local if fits_fast(mesh) else plain_local,
        mesh=mesh,
        in_specs=(
            P(("dp", "expert"), "tensor"),
            P(("dp", "expert"), None),
            P(("dp", "expert"), None),
            P(),
            P(),
            P(("dp", "expert"), "tensor"),
            P("expert", "tensor", None),
        ),
        out_specs=(P(("dp", "expert"), "tensor"), P("expert", "tensor", "dp")),
        check_vma=False,
    )
```

```python
import functools

import jax
import jax.numpy as jnp
from jax import lax
from jax.experimental import pallas as pl
from jax.experimental.pallas import tpu as pltpu
from jax.sharding import PartitionSpec as P

MESH = pl.DeviceIdType.MESH
ROW_PAIR = 2


def from_partner(x, axis, stride):
    return lax.ppermute(x, axis, [(i, i ^ 1 << stride) for i in range(lax.axis_size(axis))])


def rows_times_weight(routed_rows, weight_cols):
    return lax.dot_general(
        routed_rows, weight_cols, (((1,), (1,)), ((), ())), preferred_element_type=jnp.float32
    )


def outer_sum(activations, routed_rows):
    return lax.dot_general(
        activations, routed_rows, (((0,), (0,)), ((), ())), preferred_element_type=jnp.float32
    )


def rounded_half(term):
    return lax.optimization_barrier(term.astype(jnp.bfloat16)).astype(jnp.float32)


def plain_local(upstream, expert_ids, gate_weights, proof_lengths, advantages, hidden, down_weight):
    experts = lax.axis_size("expert")
    tok_rows = upstream.shape[0]
    top_count = expert_ids.shape[1]
    slot_rows = hidden.shape[0]
    capacity = slot_rows // experts
    block_index = lax.axis_index("dp") * experts + lax.axis_index("expert")
    positions = block_index * tok_rows + lax.iota(jnp.int32, tok_rows)
    rollout_ends = jnp.cumsum(proof_lengths)
    rollout_of = jnp.sum((positions[:, None] >= rollout_ends[None, :]).astype(jnp.int32), axis=1)
    rollout_ids = lax.iota(jnp.int32, rollout_ends.shape[0])
    token_weight = jnp.sum(
        jnp.where(
            rollout_of[:, None] == rollout_ids[None, :],
            advantages[None, :],
            jnp.zeros((), advantages.dtype),
        ),
        axis=1,
    )
    scaled = (
        (token_weight[:, None] * gate_weights)[:, :, None]
        * upstream.astype(jnp.float32)[:, None, :]
    ).astype(jnp.bfloat16)
    scaled = scaled.reshape(tok_rows * top_count, upstream.shape[1])
    flat_ids = expert_ids.reshape(-1)
    onehot = (flat_ids[:, None] == lax.iota(jnp.int32, experts)[None, :]).astype(jnp.int32)
    slot_index = jnp.sum((jnp.cumsum(onehot, axis=0) - onehot) * onehot, axis=1)
    target = flat_ids * capacity + slot_index
    outgoing = (
        jnp.zeros((experts * capacity, upstream.shape[1]), jnp.bfloat16).at[target].set(scaled)
    )
    arrived = lax.all_to_all(outgoing, "expert", split_axis=0, concat_axis=0, tiled=True)
    w_local = down_weight[0]
    model_cols = w_local.shape[1]
    routed = lax.all_gather(arrived, "tensor", axis=1, tiled=True)
    grad_hidden = rows_times_weight(routed, w_local)
    half_cols = model_cols // 2
    own_index = lax.axis_index("dp")
    partner_cols = lax.dynamic_slice_in_dim(routed, (1 - own_index) * half_cols, half_cols, 1)
    partner_rows, partner_hidden = from_partner((partner_cols, hidden), "dp", 0)
    own_cols = lax.dynamic_slice_in_dim(routed, own_index * half_cols, half_cols, 1)
    grad_shard = rounded_half(outer_sum(hidden, own_cols)) + rounded_half(
        outer_sum(partner_hidden, partner_rows)
    )
    return (grad_hidden.astype(jnp.bfloat16), grad_shard.astype(jnp.bfloat16)[None])


def fast_kernel(
    n_z, capacity, up, hid_in, w_in, ids_in, gate_in, lengths, advantages, hg_out, dg_out,
    tok, oth, hidp, hid, w, acc, hgbuf, dgbuf, routed, own_routed, ids, gates, info,
    z_send, z_recv, y_send, y_recv, b_send, c_send, c_recv, x_send, x_recv, h_send, h_recv,
    m_send, m_recv, g_send, g_recv, load_sem, store_sem, out_sem,
):
    d, e, t = lax.axis_index("dp"), lax.axis_index("expert"), lax.axis_index("tensor")
    n_e = n_z * ROW_PAIR
    z, y = e // ROW_PAIR, e % ROW_PAIR
    n_peer = 2 * n_e
    me = d * n_e + e
    cols, tok_rows = up.shape
    half = cols // 2
    couple = 2 * ROW_PAIR * capacity
    lane = couple // 3
    window = 2 * lane
    top = ids_in.shape[0]
    od, ot, ey = 1 - d, 1 - t, z * ROW_PAIR + 1 - y

    barrier = pltpu.get_barrier_semaphore()

    def greet(k, _):
        peer = (me + k) % n_peer
        pl.semaphore_signal(
            barrier, inc=1, device_id={"dp": peer // n_e, "expert": peer % n_e}, device_id_type=MESH
        )
        return 0

    lax.fori_loop(1, n_peer, greet, 0)
    pl.semaphore_signal(barrier, inc=1, device_id={"tensor": ot}, device_id_type=MESH)
    pl.semaphore_signal(
        barrier, inc=1, device_id={"dp": od, "tensor": ot}, device_id_type=MESH
    )

    loads = [
        pltpu.make_async_copy(up, tok.at[e, t], load_sem.at[0]),
        pltpu.make_async_copy(ids_in, ids.at[me], load_sem.at[1]),
        pltpu.make_async_copy(gate_in, gates.at[me], load_sem.at[4]),
        pltpu.make_async_copy(w_in, w, load_sem.at[2]),
        pltpu.make_async_copy(hid_in, hid, load_sem.at[3]),
    ]
    for load in loads:
        load.start()
    pl.semaphore_wait(barrier, n_peer + 1)

    def send(src, dst, ss, rs, where):
        return pltpu.make_async_remote_copy(
            src_ref=src, dst_ref=dst, send_sem=ss, recv_sem=rs, device_id=where, device_id_type=MESH
        )

    def x_copy(part):
        rows = pl.ds(part * half, half)
        return send(
            up.at[rows], oth.at[e, rows], x_send.at[part], x_recv.at[0], {"dp": od, "tensor": jnp.int32(part)}
        )

    @pl.when(t == od)
    def _():
        x_copy(0).start()
        x_copy(1).start()

    def m_copies(k, frm):
        peer = (me + k) % n_peer
        where = {"dp": peer // n_e, "expert": peer % n_e}
        return (
            send(ids_in, ids.at[frm], m_send.at[k], m_recv.at[k], where),
            send(gate_in, gates.at[frm], g_send.at[k], g_recv.at[k], where),
        )

    def m_start(k, _):
        for copy in m_copies(k, me):
            copy.start()
        return 0

    def slab(part, b):
        if part == 0:
            return tok.at[b, t]
        return oth.at[b, pl.ds(pl.multiple_of(t * half, half), half)]

    def z_copy(part, zz, delta, own=False):
        b = zz * ROW_PAIR + y
        src = up if own and part == 0 else slab(part, b)
        return send(
            src, slab(part, b), z_send.at[part, (delta + 1) // 2, zz], z_recv.at[part, zz],
            {"expert": (z + delta) * ROW_PAIR + y},
        )

    def y_copy(part, zz, own=False):
        b = zz * ROW_PAIR + y
        src = up if own and part == 0 else slab(part, b)
        return send(src, slab(part, b), y_send.at[part, zz], y_recv.at[part, zz], {"expert": ey})

    def y_arrival(part, zz):
        b = zz * ROW_PAIR + 1 - y
        return send(slab(part, b), slab(part, b), y_send.at[part, zz], y_recv.at[part, zz], {"expert": ey})

    def c_copy(part, b, own=False):
        src = up if own and part == 0 else slab(part, b)
        return send(src, slab(part, b), c_send.at[part, b], c_recv.at[part, b], {"tensor": ot})

    def c_arrival(part, b):
        if part == 0:
            dst = tok.at[b, ot]
        else:
            dst = oth.at[b, pl.ds(pl.multiple_of(ot * half, half), half)]
        return send(dst, dst, c_send.at[part, b], c_recv.at[part, b], {"tensor": ot})

    def pair_of(i):
        zz, bit = 0, 1
        while bit < n_z:
            zz = zz + (((z // bit) % 2 + (i // bit) % 2) % 2) * bit
            bit *= 2
        return zz

    def pair_window(zz):
        return pl.ds(pl.multiple_of((zz // 2) * couple + (zz % 2) * lane, lane), window)

    beside = pair_of(1)

    def beside_copy():
        block = slab(1, z * ROW_PAIR + 1 - y)
        return send(
            block, block, b_send.at[0], y_recv.at[1, z], {"expert": beside * ROW_PAIR + y}
        )

    def h_lanes(i, size):
        zz = pair_of(i)
        at = (zz // 2) * couple + (zz % 2) * (lane if size == window else 2 * lane)
        return pl.ds(pl.multiple_of(at, lane), size)

    def h_copy(j, size):
        lanes = h_lanes(2 * j + (0 if size == window else 1), size)
        i = 2 * j + (0 if size == window else 1)
        return send(
            hid_in.at[:, lanes], hidp.at[:, lanes], h_send.at[i], h_recv.at[i], {"dp": od}
        )

    def spread(part):
        y_copy(part, z, True).start()
        for delta in (1, -1):
            @pl.when((z + delta >= 0) & (z + delta < n_z))
            def _():
                z_copy(part, z, delta, True).start()
        c_copy(part, e, True).start()

    lax.fori_loop(1, n_peer, m_start, 0)
    spread(0)

    def h_start(j, _):
        h_copy(j, window).start()
        h_copy(j, lane).start()
        return 0

    lax.fori_loop(0, n_z // 2, h_start, 0)
    x_in = send(
        slab(1, e), slab(1, e), x_send.at[0], x_recv.at[0], {"dp": od}
    )
    x_in.wait_recv()
    spread(1)

    acc[...] = jnp.zeros_like(acc)
    hgbuf[...] = jnp.zeros_like(hgbuf)
    for load in loads:
        load.wait()

    ends, end = [], 0
    for r in range(lengths.shape[0]):
        end = end + lengths[r]
        ends.append(end)
    order = lax.broadcasted_iota(jnp.int32, (tok_rows, tok_rows), 0)
    later = lax.broadcasted_iota(jnp.int32, (tok_rows, tok_rows), 1)
    earlier = jnp.where(order < later, 1.0, 0.0).astype(jnp.bfloat16)

    def m_land(k, _):
        frm = (me + n_peer - k) % n_peer

        @pl.when(k > 0)
        def _():
            for copy in m_copies(k, frm):
                copy.wait_recv()

        named = ids[frm] == e
        token = frm * tok_rows + lax.broadcasted_iota(jnp.int32, (top, tok_rows), 1)
        rollout = jnp.zeros((top, tok_rows), jnp.int32)
        for end in ends:
            rollout = rollout + (token >= end).astype(jnp.int32)
        weight = jnp.zeros((top, tok_rows), jnp.float32)
        for r in range(lengths.shape[0]):
            weight = weight + jnp.where(rollout == r, advantages[r], 0.0)
        scale = jnp.sum(jnp.where(named, weight * gates[frm], 0.0), axis=0, keepdims=True)
        member = jnp.sum(jnp.where(named, 1.0, 0.0), axis=0, keepdims=True)
        member = jnp.broadcast_to(member, (8, tok_rows))
        before = jnp.dot(member.astype(jnp.bfloat16), earlier, preferred_element_type=jnp.float32)
        slot = jnp.where(member > 0.5, before, -float(2 * couple))
        row = lax.broadcasted_iota(jnp.int32, (8, tok_rows), 0)
        both = jnp.where(row == 0, slot, jnp.broadcast_to(scale, (8, tok_rows)))
        info[frm] = jnp.transpose(both)
        return 0

    lax.fori_loop(0, n_peer, m_land, 0)

    row_tiles = [(c, min(480, cols - c)) for c in range(0, cols, 480)]

    def picks(half_index, zz):
        base = half_index * n_e + zz * ROW_PAIR
        at = lax.broadcasted_iota(jnp.int32, (tok_rows, window), 1)
        at = (at - (zz % 2) * (couple // 2 - lane)).astype(jnp.float32)
        pick, scale = [], 0.0
        for k in range(ROW_PAIR):
            block = info[base + k]
            hit = at - k * capacity == block[:, 0:1]
            scale = scale + jnp.sum(jnp.where(hit, block[:, 1:2], 0.0), axis=0, keepdims=True)
            pick.append(jnp.where(hit, 1.0, 0.0).astype(jnp.bfloat16))
        return jnp.concatenate(pick, axis=0), scale

    def compute(i):
        zz = pair_of(i)
        slots = pair_window(zz)
        b = zz * ROW_PAIR
        pick, scale = picks(d, zz)
        opick, oscale = picks(od, zz)
        for side in range(2):
            for c, n in row_tiles:
                tokens = jnp.concatenate([tok[b + k, side, c:c + n, :] for k in range(ROW_PAIR)], axis=1)
                rows = jnp.dot(tokens, pick, preferred_element_type=jnp.float32) * scale
                routed[side * cols + c:side * cols + c + n, :] = rows.astype(jnp.bfloat16)
        for c, n in row_tiles:
            tokens = jnp.concatenate([oth[b + k, c:c + n, :] for k in range(ROW_PAIR)], axis=1)
            rows = jnp.dot(tokens, opick, preferred_element_type=jnp.float32) * oscale
            own_routed[c:c + n, window:] = rows.astype(jnp.bfloat16)
        own_routed[:, :window] = routed[pl.ds(pl.multiple_of(d * cols, 16), cols), :]
        at = lax.broadcasted_iota(jnp.int32, (1, window), 1)
        start = (zz % 2) * (couple // 2 - lane)
        mine = (at >= start) & (at < start + couple // 2)
        for c, n in row_tiles:
            rows = jnp.dot(w[c:c + n, :], routed[...], preferred_element_type=jnp.float32)
            hgbuf[c:c + n, slots] = jnp.where(mine, rows, hgbuf[c:c + n, slots].astype(jnp.float32)).astype(jnp.bfloat16)

        @pl.when(i % 2 == 1)
        def _():
            hg_store(i // 2).start()

        for parity, size in ((0, window), (1, lane)):
            @pl.when(i % 2 == parity)
            def _():
                h_copy(i // 2, size).wait_recv()

        for c, n in row_tiles:
            left = jnp.concatenate([hid[c:c + n, slots], hidp[c:c + n, slots]], axis=1)
            total = acc[c:c + n, :] + lax.dot_general(
                left, own_routed[...], (((1,), (1,)), ((), ())), preferred_element_type=jnp.float32
            )

            @pl.when(i < n_z - 1)
            def _():
                acc[c:c + n, :] = total

            @pl.when(i == n_z - 1)
            def _():
                dgbuf[c:c + n, :] = total.astype(jnp.bfloat16)
                dg_store(c, n).start()

    def dg_store(c, n):
        return pltpu.make_async_copy(
            dgbuf.at[c:c + n], dg_out.at[c:c + n], out_sem.at[c // row_tiles[0][1]]
        )

    def hg_store(j):
        lanes = pl.ds(pl.multiple_of((pair_of(2 * j) // 2) * couple, couple), couple)
        return pltpu.make_async_copy(hgbuf.at[:, lanes], hg_out.at[:, lanes], store_sem.at[j])

    def step(s, _):
        for k in (0, 1):
            delta = (1 - 2 * (z % 2)) * (1 - 2 * k)
            zz = z + delta * s

            @pl.when((s < n_z) & (zz >= 0) & (zz < n_z))
            def _():
                for part in (0, 1):
                    b = zz * ROW_PAIR + y
                    send(
                        slab(part, b), slab(part, b), z_send.at[part, 0, zz], z_recv.at[part, zz],
                        {"expert": ey},
                    ).wait_recv()

                    @pl.when((z - delta >= 0) & (z - delta < n_z))
                    def _():
                        z_copy(part, zz, -delta).start()

                    if part == 0:
                        y_copy(part, zz).start()
                    else:
                        @pl.when(zz != beside)
                        def _():
                            y_copy(part, zz).start()

                    c_copy(part, b).start()

        @pl.when(s >= 2)
        def _():
            zz = pair_of(s - 2)
            for k in range(ROW_PAIR):
                for part in (0, 1):
                    c_arrival(part, zz * ROW_PAIR + k).wait_recv()
            compute(s - 2)

        @pl.when(s <= n_z)
        def _():
            zz = pair_of(s - 1)
            for part in (0, 1):
                y_arrival(part, zz).wait_recv()
                c_copy(part, zz * ROW_PAIR + 1 - y).start()

            @pl.when(s == 1)
            def _():
                beside_copy().start()
        return 0

    lax.fori_loop(1, n_z + 2, step, 0)

    @pl.when(t == od)
    def _():
        x_copy(0).wait_send()
        x_copy(1).wait_send()

    def m_sent(k, _):
        for copy in m_copies(k, me):
            copy.wait_send()
        return 0

    lax.fori_loop(1, n_peer, m_sent, 0)

    def sent(zz, _):
        y_copy(0, zz).wait_send()

        @pl.when(zz != beside)
        def _():
            y_copy(1, zz).wait_send()

        for part in (0, 1):
            for k in range(ROW_PAIR):
                c_copy(part, zz * ROW_PAIR + k).wait_send()
            for delta in (1, -1):
                @pl.when((z + delta >= 0) & (z + delta < n_z) & ((z - zz) * delta >= 0))
                def _():
                    z_copy(part, zz, delta).wait_send()
        return 0

    lax.fori_loop(0, n_z, sent, 0)
    beside_copy().wait_send()

    def stored(j, _):
        h_copy(j, window).wait_send()
        h_copy(j, lane).wait_send()
        hg_store(j).wait()
        return 0

    lax.fori_loop(0, n_z // 2, stored, 0)
    for c, n in row_tiles:
        dg_store(c, n).wait()


def fast_local(upstream, expert_ids, gate_weights, proof_lengths, advantages, hidden, down_weight):
    n_e = lax.axis_size("expert")
    n_z = n_e // ROW_PAIR
    tok_rows, cols = upstream.shape
    slot_rows, units = hidden.shape
    capacity = slot_rows // n_e
    top = expert_ids.shape[1]
    window = 4 * ROW_PAIR * capacity // 3
    model = down_weight.shape[2]
    dma = pltpu.SemaphoreType.DMA
    bf16 = jnp.bfloat16
    hg, dg = pl.pallas_call(
        functools.partial(fast_kernel, n_z, capacity),
        out_shape=(
            jax.ShapeDtypeStruct((units, slot_rows), bf16),
            jax.ShapeDtypeStruct((units, cols), bf16),
        ),
        in_specs=[pl.BlockSpec(memory_space=pl.ANY)] * 5
        + [pl.BlockSpec(memory_space=pltpu.SMEM)] * 2,
        out_specs=(pl.BlockSpec(memory_space=pl.ANY),) * 2,
        scratch_shapes=[
            pltpu.VMEM((n_e, 2, cols, tok_rows), bf16),
            pltpu.VMEM((n_e, cols, tok_rows), bf16),
            pltpu.VMEM((units, slot_rows), bf16),
            pltpu.VMEM((units, slot_rows), bf16),
            pltpu.VMEM((units, model), bf16),
            pltpu.VMEM((units, cols), jnp.float32),
            pltpu.VMEM((units, slot_rows), bf16),
            pltpu.VMEM((units, cols), bf16),
            pltpu.VMEM((model, window), bf16),
            pltpu.VMEM((cols, 2 * window), bf16),
            pltpu.VMEM((2 * n_e, top, tok_rows), jnp.int32),
            pltpu.VMEM((2 * n_e, top, tok_rows), jnp.float32),
            pltpu.VMEM((2 * n_e, tok_rows, 8), jnp.float32),
            dma((2, 2, n_z)), dma((2, n_z)), dma((2, n_z)), dma((2, n_z)), dma((1,)),
            dma((2, n_e)), dma((2, n_e)), dma((2,)), dma((1,)), dma((n_z,)), dma((n_z,)),
            dma((2 * n_e,)), dma((2 * n_e,)), dma((2 * n_e,)), dma((2 * n_e,)), dma((5,)), dma((n_z // 2,)), dma((pl.cdiv(cols, 480),)),
        ],
        compiler_params=pltpu.CompilerParams(
            collective_id=0, has_side_effects=True, vmem_limit_bytes=60000 * 1024
        ),
    )(
        upstream.T, hidden.T, down_weight[0], expert_ids.T, gate_weights.T, proof_lengths, advantages
    )
    return hg.T, dg[None]


def fits_fast(mesh):
    n_e = mesh.shape["expert"]
    return mesh.shape["dp"] == 2 and mesh.shape["tensor"] == 2 and n_e in (4, 8, 16)


def solution(mesh):
    return jax.shard_map(
        fast_local if fits_fast(mesh) else plain_local,
        mesh=mesh,
        in_specs=(
            P(("dp", "expert"), "tensor"),
            P(("dp", "expert"), None),
            P(("dp", "expert"), None),
            P(),
            P(),
            P(("dp", "expert"), "tensor"),
            P("expert", "tensor", None),
        ),
        out_specs=(P(("dp", "expert"), "tensor"), P("expert", "tensor", "dp")),
        check_vma=False,
    )
```

```python
import functools

import jax
import jax.numpy as jnp
from jax import lax
from jax.experimental import pallas as pl
from jax.experimental.pallas import tpu as pltpu
from jax.sharding import PartitionSpec as P

MESH = pl.DeviceIdType.MESH
ROW_PAIR = 2


def from_partner(x, axis, stride):
    return lax.ppermute(x, axis, [(i, i ^ 1 << stride) for i in range(lax.axis_size(axis))])


def rows_times_weight(routed_rows, weight_cols):
    return lax.dot_general(
        routed_rows, weight_cols, (((1,), (1,)), ((), ())), preferred_element_type=jnp.float32
    )


def outer_sum(activations, routed_rows):
    return lax.dot_general(
        activations, routed_rows, (((0,), (0,)), ((), ())), preferred_element_type=jnp.float32
    )


def rounded_half(term):
    return lax.optimization_barrier(term.astype(jnp.bfloat16)).astype(jnp.float32)


def plain_local(upstream, expert_ids, gate_weights, proof_lengths, advantages, hidden, down_weight):
    experts = lax.axis_size("expert")
    tok_rows = upstream.shape[0]
    top_count = expert_ids.shape[1]
    slot_rows = hidden.shape[0]
    capacity = slot_rows // experts
    block_index = lax.axis_index("dp") * experts + lax.axis_index("expert")
    positions = block_index * tok_rows + lax.iota(jnp.int32, tok_rows)
    rollout_ends = jnp.cumsum(proof_lengths)
    rollout_of = jnp.sum((positions[:, None] >= rollout_ends[None, :]).astype(jnp.int32), axis=1)
    rollout_ids = lax.iota(jnp.int32, rollout_ends.shape[0])
    token_weight = jnp.sum(
        jnp.where(
            rollout_of[:, None] == rollout_ids[None, :],
            advantages[None, :],
            jnp.zeros((), advantages.dtype),
        ),
        axis=1,
    )
    scaled = (
        (token_weight[:, None] * gate_weights)[:, :, None]
        * upstream.astype(jnp.float32)[:, None, :]
    ).astype(jnp.bfloat16)
    scaled = scaled.reshape(tok_rows * top_count, upstream.shape[1])
    flat_ids = expert_ids.reshape(-1)
    onehot = (flat_ids[:, None] == lax.iota(jnp.int32, experts)[None, :]).astype(jnp.int32)
    slot_index = jnp.sum((jnp.cumsum(onehot, axis=0) - onehot) * onehot, axis=1)
    target = flat_ids * capacity + slot_index
    outgoing = (
        jnp.zeros((experts * capacity, upstream.shape[1]), jnp.bfloat16).at[target].set(scaled)
    )
    arrived = lax.all_to_all(outgoing, "expert", split_axis=0, concat_axis=0, tiled=True)
    w_local = down_weight[0]
    model_cols = w_local.shape[1]
    routed = lax.all_gather(arrived, "tensor", axis=1, tiled=True)
    grad_hidden = rows_times_weight(routed, w_local)
    half_cols = model_cols // 2
    own_index = lax.axis_index("dp")
    partner_cols = lax.dynamic_slice_in_dim(routed, (1 - own_index) * half_cols, half_cols, 1)
    partner_rows, partner_hidden = from_partner((partner_cols, hidden), "dp", 0)
    own_cols = lax.dynamic_slice_in_dim(routed, own_index * half_cols, half_cols, 1)
    grad_shard = rounded_half(outer_sum(hidden, own_cols)) + rounded_half(
        outer_sum(partner_hidden, partner_rows)
    )
    return (grad_hidden.astype(jnp.bfloat16), grad_shard.astype(jnp.bfloat16)[None])


def fast_kernel(
    n_z, capacity, up, hid_in, w_in, ids_in, gate_in, lengths, advantages, hg_out, dg_out,
    tok, oth, hidp, hid, w, acc, hgbuf, dgbuf, routed, own_routed, ids, gates, info,
    z_send, z_recv, y_send, y_recv, b_send, c_send, c_recv, x_send, x_recv, h_send, h_recv,
    m_send, m_recv, g_send, g_recv, load_sem, store_sem, out_sem,
):
    d, e, t = lax.axis_index("dp"), lax.axis_index("expert"), lax.axis_index("tensor")
    n_e = n_z * ROW_PAIR
    z, y = e // ROW_PAIR, e % ROW_PAIR
    n_peer = 2 * n_e
    me = d * n_e + e
    cols, tok_rows = up.shape
    half = cols // 2
    couple = 2 * ROW_PAIR * capacity
    lane = couple // 3
    window = 2 * lane
    top = ids_in.shape[0]
    od, ot, ey = 1 - d, 1 - t, z * ROW_PAIR + 1 - y

    barrier = pltpu.get_barrier_semaphore()

    def greet(k, _):
        peer = (me + k) % n_peer
        pl.semaphore_signal(
            barrier, inc=1, device_id={"dp": peer // n_e, "expert": peer % n_e}, device_id_type=MESH
        )
        return 0

    lax.fori_loop(1, n_peer, greet, 0)
    pl.semaphore_signal(barrier, inc=1, device_id={"tensor": ot}, device_id_type=MESH)
    pl.semaphore_signal(
        barrier, inc=1, device_id={"dp": od, "tensor": ot}, device_id_type=MESH
    )

    loads = [
        pltpu.make_async_copy(up, tok.at[e, t], load_sem.at[0]),
        pltpu.make_async_copy(ids_in, ids.at[me], load_sem.at[1]),
        pltpu.make_async_copy(gate_in, gates.at[me], load_sem.at[4]),
        pltpu.make_async_copy(w_in, w, load_sem.at[2]),
        pltpu.make_async_copy(hid_in, hid, load_sem.at[3]),
    ]
    for load in loads:
        load.start()
    pl.semaphore_wait(barrier, n_peer + 1)

    def send(src, dst, ss, rs, where):
        return pltpu.make_async_remote_copy(
            src_ref=src, dst_ref=dst, send_sem=ss, recv_sem=rs, device_id=where, device_id_type=MESH
        )

    def x_copy(part):
        rows = pl.ds(part * half, half)
        return send(
            up.at[rows], oth.at[e, rows], x_send.at[part], x_recv.at[0], {"dp": od, "tensor": jnp.int32(part)}
        )

    @pl.when(t == od)
    def _():
        x_copy(0).start()
        x_copy(1).start()

    def m_copies(k, frm):
        peer = (me + k) % n_peer
        where = {"dp": peer // n_e, "expert": peer % n_e}
        return (
            send(ids_in, ids.at[frm], m_send.at[k], m_recv.at[k], where),
            send(gate_in, gates.at[frm], g_send.at[k], g_recv.at[k], where),
        )

    def m_start(k, _):
        for copy in m_copies(k, me):
            copy.start()
        return 0

    def slab(part, b):
        if part == 0:
            return tok.at[b, t]
        return oth.at[b, pl.ds(pl.multiple_of(t * half, half), half)]

    def z_copy(part, zz, delta, own=False):
        b = zz * ROW_PAIR + y
        src = up if own and part == 0 else slab(part, b)
        return send(
            src, slab(part, b), z_send.at[part, (delta + 1) // 2, zz], z_recv.at[part, zz],
            {"expert": (z + delta) * ROW_PAIR + y},
        )

    def y_copy(part, zz, own=False):
        b = zz * ROW_PAIR + y
        src = up if own and part == 0 else slab(part, b)
        return send(src, slab(part, b), y_send.at[part, zz], y_recv.at[part, zz], {"expert": ey})

    def y_arrival(part, zz):
        b = zz * ROW_PAIR + 1 - y
        return send(slab(part, b), slab(part, b), y_send.at[part, zz], y_recv.at[part, zz], {"expert": ey})

    def c_copy(part, b, own=False):
        src = up if own and part == 0 else slab(part, b)
        return send(src, slab(part, b), c_send.at[part, b], c_recv.at[part, b], {"tensor": ot})

    def c_arrival(part, b):
        if part == 0:
            dst = tok.at[b, ot]
        else:
            dst = oth.at[b, pl.ds(pl.multiple_of(ot * half, half), half)]
        return send(dst, dst, c_send.at[part, b], c_recv.at[part, b], {"tensor": ot})

    def pair_of(i):
        zz, bit = 0, 1
        while bit < n_z:
            zz = zz + (((z // bit) % 2 + (i // bit) % 2) % 2) * bit
            bit *= 2
        return zz

    def pair_window(zz):
        return pl.ds(pl.multiple_of((zz // 2) * couple + (zz % 2) * lane, lane), window)

    beside = pair_of(1)
    inner = (z > 0) & (z < n_z - 1)

    def beside_copy():
        block = slab(1, z * ROW_PAIR + 1 - y)
        return send(
            block, block, b_send.at[0], y_recv.at[1, z], {"expert": beside * ROW_PAIR + y}
        )

    def h_lanes(i, size):
        zz = pair_of(i)
        at = (zz // 2) * couple + (zz % 2) * (lane if size == window else 2 * lane)
        return pl.ds(pl.multiple_of(at, lane), size)

    def h_copy(j, size):
        lanes = h_lanes(2 * j + (0 if size == window else 1), size)
        i = 2 * j + (0 if size == window else 1)
        return send(
            hid_in.at[:, lanes], hidp.at[:, lanes], h_send.at[i], h_recv.at[i], {"dp": od}
        )

    def spread(part):
        y_copy(part, z, True).start()
        for delta in (1, -1):
            @pl.when((z + delta >= 0) & (z + delta < n_z))
            def _():
                z_copy(part, z, delta, True).start()
        c_copy(part, e, True).start()

    lax.fori_loop(1, n_peer, m_start, 0)
    spread(0)

    def h_start(j, _):
        h_copy(j, window).start()
        h_copy(j, lane).start()
        return 0

    lax.fori_loop(0, n_z // 2, h_start, 0)
    x_in = send(
        slab(1, e), slab(1, e), x_send.at[0], x_recv.at[0], {"dp": od}
    )
    x_in.wait_recv()
    spread(1)

    ends, end = [], 0
    for r in range(lengths.shape[0]):
        end = end + lengths[r]
        ends.append(end)
    order = lax.broadcasted_iota(jnp.int32, (tok_rows, tok_rows), 0)
    later = lax.broadcasted_iota(jnp.int32, (tok_rows, tok_rows), 1)
    earlier = jnp.where(order < later, 1.0, 0.0).astype(jnp.bfloat16)

    def m_land(k, _):
        frm = (me + n_peer - k) % n_peer

        @pl.when(k > 0)
        def _():
            for copy in m_copies(k, frm):
                copy.wait_recv()

        named = ids[frm] == e
        token = frm * tok_rows + lax.broadcasted_iota(jnp.int32, (top, tok_rows), 1)
        rollout = jnp.zeros((top, tok_rows), jnp.int32)
        for end in ends:
            rollout = rollout + (token >= end).astype(jnp.int32)
        weight = jnp.zeros((top, tok_rows), jnp.float32)
        for r in range(lengths.shape[0]):
            weight = weight + jnp.where(rollout == r, advantages[r], 0.0)
        scale = jnp.sum(jnp.where(named, weight * gates[frm], 0.0), axis=0, keepdims=True)
        member = jnp.sum(jnp.where(named, 1.0, 0.0), axis=0, keepdims=True)
        member = jnp.broadcast_to(member, (8, tok_rows))
        before = jnp.dot(member.astype(jnp.bfloat16), earlier, preferred_element_type=jnp.float32)
        slot = jnp.where(member > 0.5, before, -float(2 * couple))
        row = lax.broadcasted_iota(jnp.int32, (8, tok_rows), 0)
        both = jnp.where(row == 0, slot, jnp.broadcast_to(scale, (8, tok_rows)))
        info[frm] = jnp.transpose(both)
        return 0


    row_tiles = [(c, min(480, cols - c)) for c in range(0, cols, 480)]

    def picks(half_index, zz):
        base = half_index * n_e + zz * ROW_PAIR
        at = lax.broadcasted_iota(jnp.int32, (tok_rows, window), 1)
        at = (at - (zz % 2) * (couple // 2 - lane)).astype(jnp.float32)
        pick, scale = [], 0.0
        for k in range(ROW_PAIR):
            block = info[base + k]
            hit = at - k * capacity == block[:, 0:1]
            scale = scale + jnp.sum(jnp.where(hit, block[:, 1:2], 0.0), axis=0, keepdims=True)
            pick.append(jnp.where(hit, 1.0, 0.0).astype(jnp.bfloat16))
        return jnp.concatenate(pick, axis=0), scale

    def compute(i):
        zz = pair_of(i)
        slots = pair_window(zz)
        b = zz * ROW_PAIR
        pick, scale = picks(d, zz)
        opick, oscale = picks(od, zz)
        for side in range(2):
            for c, n in row_tiles:
                tokens = jnp.concatenate([tok[b + k, side, c:c + n, :] for k in range(ROW_PAIR)], axis=1)
                rows = jnp.dot(tokens, pick, preferred_element_type=jnp.float32) * scale
                routed[side * cols + c:side * cols + c + n, :] = rows.astype(jnp.bfloat16)
        for c, n in row_tiles:
            tokens = jnp.concatenate([oth[b + k, c:c + n, :] for k in range(ROW_PAIR)], axis=1)
            rows = jnp.dot(tokens, opick, preferred_element_type=jnp.float32) * oscale
            own_routed[c:c + n, window:] = rows.astype(jnp.bfloat16)
        own_routed[:, :window] = routed[pl.ds(pl.multiple_of(d * cols, 16), cols), :]
        at = lax.broadcasted_iota(jnp.int32, (1, window), 1)
        start = (zz % 2) * (couple // 2 - lane)
        mine = (at >= start) & (at < start + couple // 2)
        for c, n in row_tiles:
            rows = jnp.dot(w[c:c + n, :], routed[...], preferred_element_type=jnp.float32)
            hgbuf[c:c + n, slots] = jnp.where(mine, rows, hgbuf[c:c + n, slots].astype(jnp.float32)).astype(jnp.bfloat16)

        @pl.when(i % 2 == 1)
        def _():
            hg_store(i // 2).start()

        for parity, size in ((0, window), (1, lane)):
            @pl.when(i % 2 == parity)
            def _():
                h_copy(i // 2, size).wait_recv()

        def summed(c, n):
            left = jnp.concatenate([hid[c:c + n, slots], hidp[c:c + n, slots]], axis=1)
            return acc[c:c + n, :] + lax.dot_general(
                left, own_routed[...], (((1,), (1,)), ((), ())), preferred_element_type=jnp.float32
            )

        @pl.when(i < n_z - 1)
        def _():
            for c, n in row_tiles:
                acc[c:c + n, :] = summed(c, n)

        @pl.when(i == n_z - 1)
        def _():
            for c, n in row_tiles:
                dgbuf[c:c + n, :] = summed(c, n).astype(jnp.bfloat16)
                dg_store(c, n).start()

    def dg_store(c, n):
        return pltpu.make_async_copy(
            dgbuf.at[c:c + n], dg_out.at[c:c + n], out_sem.at[c // row_tiles[0][1]]
        )

    def hg_store(j):
        lanes = pl.ds(pl.multiple_of((pair_of(2 * j) // 2) * couple, couple), couple)
        return pltpu.make_async_copy(hgbuf.at[:, lanes], hg_out.at[:, lanes], store_sem.at[j])

    def step(s, _):
        for k in (0, 1):
            delta = (1 - 2 * (z % 2)) * (1 - 2 * k)
            zz = z + delta * s

            @pl.when((s < n_z) & (zz >= 0) & (zz < n_z))
            def _():
                for part in (0, 1):
                    b = zz * ROW_PAIR + y
                    send(
                        slab(part, b), slab(part, b), z_send.at[part, 0, zz], z_recv.at[part, zz],
                        {"expert": ey},
                    ).wait_recv()

                    @pl.when((z - delta >= 0) & (z - delta < n_z))
                    def _():
                        z_copy(part, zz, -delta).start()

                    if part == 0:
                        y_copy(part, zz).start()
                    else:
                        @pl.when((zz != beside) | ~inner)
                        def _():
                            y_copy(part, zz).start()

                    c_copy(part, b).start()

        @pl.when(s == 1)
        def _():
            for load in loads:
                load.wait()
            lax.fori_loop(0, n_peer, m_land, 0)
            hgbuf[...] = jnp.zeros_like(hgbuf)
            acc[...] = jnp.zeros_like(acc)

        @pl.when(s >= 2)
        def _():
            zz = pair_of(s - 2)
            for k in range(ROW_PAIR):
                for part in (0, 1):
                    c_arrival(part, zz * ROW_PAIR + k).wait_recv()
            compute(s - 2)

        @pl.when(s <= n_z)
        def _():
            zz = pair_of(s - 1)
            for part in (0, 1):
                y_arrival(part, zz).wait_recv()
                c_copy(part, zz * ROW_PAIR + 1 - y).start()

            @pl.when((s == 1) & ~inner)
            def _():
                beside_copy().start()
        return 0

    lax.fori_loop(1, n_z + 2, step, 0)

    @pl.when(t == od)
    def _():
        x_copy(0).wait_send()
        x_copy(1).wait_send()

    def m_sent(k, _):
        for copy in m_copies(k, me):
            copy.wait_send()
        return 0

    lax.fori_loop(1, n_peer, m_sent, 0)

    def sent(zz, _):
        y_copy(0, zz).wait_send()

        @pl.when((zz != beside) | ~inner)
        def _():
            y_copy(1, zz).wait_send()

        for part in (0, 1):
            for k in range(ROW_PAIR):
                c_copy(part, zz * ROW_PAIR + k).wait_send()
            for delta in (1, -1):
                @pl.when((z + delta >= 0) & (z + delta < n_z) & ((z - zz) * delta >= 0))
                def _():
                    z_copy(part, zz, delta).wait_send()
        return 0

    lax.fori_loop(0, n_z, sent, 0)

    @pl.when(~inner)
    def _():
        beside_copy().wait_send()


    def stored(j, _):
        h_copy(j, window).wait_send()
        h_copy(j, lane).wait_send()
        hg_store(j).wait()
        return 0

    lax.fori_loop(0, n_z // 2, stored, 0)
    for c, n in row_tiles:
        dg_store(c, n).wait()


def fast_local(upstream, expert_ids, gate_weights, proof_lengths, advantages, hidden, down_weight):
    n_e = lax.axis_size("expert")
    n_z = n_e // ROW_PAIR
    tok_rows, cols = upstream.shape
    slot_rows, units = hidden.shape
    capacity = slot_rows // n_e
    top = expert_ids.shape[1]
    window = 4 * ROW_PAIR * capacity // 3
    model = down_weight.shape[2]
    dma = pltpu.SemaphoreType.DMA
    bf16 = jnp.bfloat16
    hg, dg = pl.pallas_call(
        functools.partial(fast_kernel, n_z, capacity),
        out_shape=(
            jax.ShapeDtypeStruct((units, slot_rows), bf16),
            jax.ShapeDtypeStruct((units, cols), bf16),
        ),
        in_specs=[pl.BlockSpec(memory_space=pl.ANY)] * 5
        + [pl.BlockSpec(memory_space=pltpu.SMEM)] * 2,
        out_specs=(pl.BlockSpec(memory_space=pl.ANY),) * 2,
        scratch_shapes=[
            pltpu.VMEM((n_e, 2, cols, tok_rows), bf16),
            pltpu.VMEM((n_e, cols, tok_rows), bf16),
            pltpu.VMEM((units, slot_rows), bf16),
            pltpu.VMEM((units, slot_rows), bf16),
            pltpu.VMEM((units, model), bf16),
            pltpu.VMEM((units, cols), jnp.float32),
            pltpu.VMEM((units, slot_rows), bf16),
            pltpu.VMEM((units, cols), bf16),
            pltpu.VMEM((model, window), bf16),
            pltpu.VMEM((cols, 2 * window), bf16),
            pltpu.VMEM((2 * n_e, top, tok_rows), jnp.int32),
            pltpu.VMEM((2 * n_e, top, tok_rows), jnp.float32),
            pltpu.VMEM((2 * n_e, tok_rows, 8), jnp.float32),
            dma((2, 2, n_z)), dma((2, n_z)), dma((2, n_z)), dma((2, n_z)), dma((1,)),
            dma((2, n_e)), dma((2, n_e)), dma((2,)), dma((1,)), dma((n_z,)), dma((n_z,)),
            dma((2 * n_e,)), dma((2 * n_e,)), dma((2 * n_e,)), dma((2 * n_e,)), dma((5,)), dma((n_z // 2,)), dma((pl.cdiv(cols, 480),)),
        ],
        compiler_params=pltpu.CompilerParams(
            collective_id=0, has_side_effects=True, vmem_limit_bytes=60000 * 1024
        ),
    )(
        upstream.T, hidden.T, down_weight[0], expert_ids.T, gate_weights.T, proof_lengths, advantages
    )
    return hg.T, dg[None]


def fits_fast(mesh):
    n_e = mesh.shape["expert"]
    return mesh.shape["dp"] == 2 and mesh.shape["tensor"] == 2 and n_e == 4 * ROW_PAIR


def solution(mesh):
    return jax.shard_map(
        fast_local if fits_fast(mesh) else plain_local,
        mesh=mesh,
        in_specs=(
            P(("dp", "expert"), "tensor"),
            P(("dp", "expert"), None),
            P(("dp", "expert"), None),
            P(),
            P(),
            P(("dp", "expert"), "tensor"),
            P("expert", "tensor", None),
        ),
        out_specs=(P(("dp", "expert"), "tensor"), P("expert", "tensor", "dp")),
        check_vma=False,
    )
```
